32 devices in a mesh: blk: 8 (over z, y), bins: 4 (over x, core).
Axes of the slice: x: 2, y: 2, z: 4, core: 2. Of those that a mesh axis runs over, the one named last changes fastest.
Arguments:
- density: float32 [128, 32768], P('bins', 'blk'), may hold values from 0.05 to 3
- courant: float32 [128, 32768], P('bins', 'blk'), may hold values from -0.5 to 0.3
- gain_tables: float32 [4, 8, 64, 1024], P('bins'), may hold values from -0.0625 to 0.0625
- sources: int32 [4, 8], P('bins'), may hold values from 0 to 3, as said below
- counts: int32 [4], P('bins'), may hold values from 1 to 8, as said below
- targets: int32 [4, 64], P('bins'), may hold values from 0 to 63, each once within a row
- overflow: int32 [4], replicated, may hold values from 1 to 3, as said below
Outputs:
- updated: float32 [128, 32768], P('bins', 'blk')
The draws below stay inside these ranges and needn't reach their ends.
Inputs may be any that keep to these rules, and one draw needn't show every extreme that they name: sources[g][0] is g; every other entry of row g lies in max(0, g - 2) to g. counts[0] is 1 and counts[3] is 8. `targets`: each row is a permutation of 0 to 63. overflow[0] is 1; for 0 < g < 3, overflow[g] is g + 1 or g + 2, capped at 3; overflow[3] is 3.
All inputs are finite; a program needn't handle non-finite values.
Results may differ from the reference program's by a relative error of at most 0.0003.
Values sent between devices are 32-bit elements; how exact they have to be, the bound alone decides.
A program may use at most 64 MiB of HBM per device.

```python
import math
import jax
import jax.numpy as jnp
from jax import lax

GROUP_BINS = 32
SOURCES = 8
CELLS_DEV = 4096
GROUPS = 4
BINS = 128
PAIRS = 1024
TARGETS = 64
SPAN = 2
CELLS = 32768


def draw_sources(key, part):
    own_group = jnp.arange(GROUPS, dtype=jnp.int32)
    lowest = jnp.maximum(own_group - SPAN, 0)
    choices_count = own_group - lowest + 1
    raw_bits = jax.random.randint(key, (GROUPS, SOURCES - 1), 0, 1 << 20, dtype=jnp.int32)
    picked = lowest[:, None] + raw_bits % choices_count[:, None]
    return jnp.concatenate([own_group[:, None], picked], axis=1).astype(jnp.int32)


def draw_counts(key, part):
    raw_counts = jax.random.randint(key, (GROUPS,), 1, SOURCES + 1, dtype=jnp.int32)
    return raw_counts.at[0].set(1).at[GROUPS - 1].set(SOURCES).astype(jnp.int32)


def draw_overflow(key, part):
    own_group = jnp.arange(GROUPS, dtype=jnp.int32)
    jumps = jax.random.randint(key, (GROUPS,), 1, 3, dtype=jnp.int32)
    jumps = jumps.at[0].set(1)
    return jnp.minimum(own_group + jumps, GROUPS - 1).astype(jnp.int32)


def block_scale(rng, extent, pieces, least, high):
    def one(axis_at, parts):
        heights = jax.random.uniform(jax.random.fold_in(jax.random.fold_in(rng, 6), axis_at), (parts,), jnp.float32, least / len(pieces), high / len(pieces))
        return jnp.repeat(jnp.exp(heights), extent[axis_at] // parts).reshape((-1,) + (1,) * (len(extent) - axis_at - 1))

    level = one(*pieces[0])
    for cut in pieces[1:]:
        level = level * one(*cut)
    return level


def normal_values(key, extent, deviation, reach, shards=(), held_as=jnp.bfloat16):
    drawn = jax.random.normal(key, extent, jnp.float32) * deviation
    if len(shards) > 0:
        drawn = block_scale(key, extent, shards, -0.22, 0.18) * drawn
    return jnp.clip(drawn, min=-reach, max=reach).astype(held_as)


def setup_inputs(seed: int = 0) -> dict:
    splits = jax.random.split(jax.random.key(seed), 8)
    return {
        "density": jnp.clip(jnp.exp(math.log(3.0) - 4.0943445 * jax.random.uniform(splits[0], (BINS, CELLS), jnp.float32) ** block_scale(splits[0], (BINS, CELLS), ((0, 4), (1, 8)), -0.2, 0.2)), 0.05, 3.0),
        "courant": jnp.clip(-0.5 + 0.8 * jax.random.uniform(splits[1], (BINS, CELLS), jnp.float32) ** block_scale(splits[1], (BINS, CELLS), ((0, 4), (1, 8)), -0.2, 0.2), -0.5, 0.3),
        "gain_tables": normal_values(splits[2], (GROUPS, SOURCES, TARGETS, PAIRS), (SOURCES * PAIRS) ** -0.5, 0.0625, ((0, 4),), jnp.float32),
        "sources": draw_sources(jax.random.fold_in(splits[7], 71), 0),
        "counts": draw_counts(jax.random.fold_in(splits[7], 71), 0),
        "targets": jax.vmap(lambda own: jax.random.permutation(own, TARGETS))(jax.random.split(splits[5], GROUPS)).reshape((GROUPS, TARGETS)).astype(jnp.int32),
        "overflow": draw_overflow(jax.random.fold_in(splits[7], 71), 0),
    }


RATE = 0.5


def minmod(first, second):
    agree = first * second > 0.0
    smaller = jnp.where(first > 0.0, jnp.minimum(first, second), jnp.maximum(first, second))
    return jnp.where(agree, smaller, jnp.zeros_like(first))


def advect(padded, speeds):
    width = padded.shape[1] - 4
    slopes = minmod(padded[:, 1:-1] - padded[:, :-2], padded[:, 2:] - padded[:, 1:-1])
    left_state = padded[:, 1:width + 2] + 0.5 * slopes[:, 0:width + 1]
    right_state = padded[:, 2:width + 3] - 0.5 * slopes[:, 1:width + 2]
    face_speed = speeds[:, 2:width + 3]
    face_flux = jnp.where(face_speed > 0.0, face_speed * left_state, face_speed * right_state)
    return padded[:, 2:width + 2] - (face_flux[:, 1:] - face_flux[:, :-1])


def outer_pairs(own_block, src_block):
    return (own_block[:, None, :] * src_block[None, :, :]).reshape(-1, own_block.shape[1])


def reference(density, courant, gain_tables, sources, counts, targets, overflow):
    advected = advect(jnp.pad(density, ((0, 0), (2, 2))), jnp.pad(courant, ((0, 0), (2, 2))))
    grouped = advected.reshape(GROUPS, GROUP_BINS, CELLS)
    block_count = CELLS // CELLS_DEV

    def per_group(own_group):
        own_rows = grouped[own_group]

        def per_block(block_index):
            first_row = (block_index * CELLS_DEV).astype(jnp.int32)
            own_block = lax.dynamic_slice_in_dim(own_rows, first_row, CELLS_DEV, 1)
            summed = jnp.zeros((TARGETS, CELLS_DEV), jnp.float32)
            for slot in range(SOURCES):
                src_block = lax.dynamic_slice_in_dim(grouped[sources[own_group, slot]], first_row, CELLS_DEV, 1)
                active = (slot < counts[own_group]).astype(jnp.float32)
                summed = summed + active * jnp.dot(gain_tables[own_group, slot], outer_pairs(own_block, src_block), precision=lax.Precision.HIGHEST)
            return summed

        blocks = lax.map(per_block, jnp.arange(block_count, dtype=jnp.int32))
        result = blocks.transpose(1, 0, 2).reshape(TARGETS, CELLS)
        placement = (targets[own_group][None, :] == jnp.arange(TARGETS, dtype=jnp.int32)[:, None]).astype(jnp.float32)
        return jnp.dot(placement, result, precision=lax.Precision.HIGHEST)

    placed = lax.map(per_group, jnp.arange(GROUPS, dtype=jnp.int32))
    own_gain = placed[:, :GROUP_BINS]
    spill = placed[:, GROUP_BINS:]
    routing = (overflow[None, :] == jnp.arange(GROUPS, dtype=jnp.int32)[:, None]).astype(jnp.float32)
    received = jnp.einsum("gh,hbc->gbc", routing, spill, precision=lax.Precision.HIGHEST)
    return (grouped + RATE * (own_gain + received)).reshape(BINS, CELLS)
```

```python
import functools

import jax
import jax.numpy as jnp
from jax import lax
from jax.experimental import pallas as pl
from jax.experimental.pallas import tpu as pltpu
from jax.sharding import PartitionSpec as P

RATE = 0.5
EDGE = 128
CHUNK = 512
HALF = 256
MESH = pl.DeviceIdType.MESH


def minmod(first, second):
    agree = first * second > 0.0
    smaller = jnp.where(first > 0.0, jnp.minimum(first, second), jnp.maximum(first, second))
    return jnp.where(agree, smaller, jnp.zeros_like(first))


def advect_window(cells, speeds):
    width = cells.shape[1]
    diff = cells - pltpu.roll(cells, 1, 1)
    slopes = minmod(diff, pltpu.roll(diff, width - 1, 1))
    left_state = pltpu.roll(cells + 0.5 * slopes, 1, 1)
    right_state = cells - 0.5 * slopes
    flux = jnp.where(speeds > 0.0, speeds * left_state, speeds * right_state)
    moved = cells - (pltpu.roll(flux, width - 1, 1) - flux)
    return moved[:, EDGE : width - EDGE]


def kernel(
    span, group_count, blk_count,
    density, courant, tables, sources, counts, targets, overflow,
    out,
    dpad, upad, tab, adv, spill, parts, lmat,
    load_sem, halo_send, halo_recv, direct_sem, sib_sem, adv_recv,
    sdirect_sem, ssib_sem, spill_recv,
):
    g = lax.axis_index("bins")
    b = lax.axis_index("blk")
    rows, width = density.shape
    chunks = width // CHUNK
    slots = tables.shape[1]
    target_count = tables.shape[2]
    reach = span + 1
    even = lax.rem(g, 2) == 0
    has_left, has_right = b > 0, b < blk_count - 1

    loads = [
        pltpu.make_async_copy(density, dpad.at[:, pl.ds(EDGE, width)], load_sem.at[0]),
        pltpu.make_async_copy(courant, upad.at[:, pl.ds(EDGE, width)], load_sem.at[1]),
        pltpu.make_async_copy(tables.at[0], tab, load_sem.at[2]),
    ]
    for load in loads:
        load.start()

    barrier = pltpu.get_barrier_semaphore()
    expected = jnp.int32(0)
    for step in [s for s in range(-span, span + 1) if s != 0]:
        there = (g + step >= 0) & (g + step < group_count)
        expected = expected + there.astype(jnp.int32)

        @pl.when(there)
        def _():
            pl.semaphore_signal(barrier, inc=1, device_id={"bins": g + step}, device_id_type=MESH)

    for step, there in ((-1, has_left), (1, has_right)):
        expected = expected + there.astype(jnp.int32)

        @pl.when(there)
        def _():
            pl.semaphore_signal(barrier, inc=1, device_id={"blk": b + step}, device_id_type=MESH)

    zero_edge = jnp.zeros((rows, EDGE), jnp.float32)
    upad[:, pl.ds(0, EDGE)] = zero_edge

    @pl.when(jnp.logical_not(has_left))
    def _():
        dpad[:, pl.ds(0, EDGE)] = zero_edge

    @pl.when(jnp.logical_not(has_right))
    def _():
        dpad[:, pl.ds(EDGE + width, EDGE)] = zero_edge
        upad[:, pl.ds(EDGE + width, EDGE)] = zero_edge

    for distance in range(1, reach):

        @pl.when(g < distance)
        def _():
            adv[distance] = jnp.zeros((rows, width), jnp.float32)

    pl.semaphore_wait(barrier, expected)

    def remote(src, dst, send, recv, where):
        return pltpu.make_async_remote_copy(
            src_ref=src, dst_ref=dst, send_sem=send, recv_sem=recv,
            device_id=where, device_id_type=MESH,
        )

    to_right = remote(
        density.at[:, pl.ds(width - EDGE, EDGE)], dpad.at[:, pl.ds(0, EDGE)],
        halo_send.at[0], halo_recv.at[0], {"blk": b + 1},
    )
    to_left = remote(
        density.at[:, pl.ds(0, EDGE)], dpad.at[:, pl.ds(EDGE + width, EDGE)],
        halo_send.at[1], halo_recv.at[1], {"blk": b - 1},
    )
    speed_left = remote(
        courant.at[:, pl.ds(0, EDGE)], upad.at[:, pl.ds(EDGE + width, EDGE)],
        halo_send.at[2], halo_recv.at[2], {"blk": b - 1},
    )

    @pl.when(has_right)
    def _():
        to_right.start()

    @pl.when(has_left)
    def _():
        to_left.start()
        speed_left.start()

    def window(k):
        return pl.ds(pl.multiple_of(k * CHUNK, CHUNK), CHUNK)

    def adv_direct(distance, k):
        return remote(
            adv.at[0, :, window(k)], adv.at[distance, :, window(k)],
            direct_sem.at[distance - 1, k], adv_recv.at[distance - 1, k], {"bins": g + distance},
        )

    def adv_sib(distance, k):
        return remote(
            adv.at[distance - 1, :, window(k)], adv.at[distance, :, window(k)],
            sib_sem.at[distance - 1, k], adv_recv.at[distance - 1, k], {"bins": g + 1},
        )

    def spill_direct(distance, k):
        return remote(
            spill.at[0, :, window(k)], spill.at[distance, :, window(k)],
            sdirect_sem.at[distance - 1, k], spill_recv.at[distance - 1, k], {"bins": g + distance},
        )

    def spill_sib(distance, k):
        return remote(
            spill.at[distance - 1, :, window(k)], spill.at[distance, :, window(k)],
            ssib_sem.at[distance - 1, k], spill_recv.at[distance - 1, k], {"bins": g + 1},
        )

    def sends_direct(distance):
        target = g + distance
        return (target < group_count) & (lax.rem(target, 2) == 0)

    def sends_sib(distance):
        return even & (g + 1 < group_count) & (g >= distance - 1)

    def spills_direct(distance):
        target = g + distance
        fits = (target < group_count) & (lax.rem(target, 2) == 0)
        return fits & (g > 0) if distance > 1 else fits

    def spills_sib(distance):
        fits = even & (g + 1 < group_count)
        return fits & (g > 1) if distance > 1 else fits

    def spill_arrives(distance):
        return g >= (1 if distance == 1 else 3)

    loads[0].wait()
    loads[1].wait()

    @pl.loop(0, chunks)
    def _(c):
        k = lax.rem(c + 1, chunks)

        @pl.when(c == chunks - 2)
        def _():
            @pl.when(has_left)
            def _():
                to_right.wait_recv()

            @pl.when(has_right)
            def _():
                to_left.wait_recv()
                speed_left.wait_recv()

        padded = pl.ds(pl.multiple_of(k * CHUNK, CHUNK), CHUNK + 2 * EDGE)
        adv[0, :, window(k)] = advect_window(dpad[:, padded], upad[:, padded])
        for distance in range(1, reach):

            @pl.when(sends_direct(distance))
            def _():
                adv_direct(distance, k).start()

        @pl.when(sends_sib(1))
        def _():
            adv_sib(1, k).start()

    loads[2].wait()
    place = (
        lax.broadcasted_iota(jnp.int32, (target_count, target_count), 0) == targets[...]
    ).astype(jnp.float32).astype(jnp.bfloat16)
    weights = [
        [
            jnp.where((sources[0, slot] == g - distance) & (slot < counts[0]), 1.0, 0.0)
            for slot in range(slots)
        ]
        for distance in range(reach)
    ]
    pair_count = tab.shape[2]

    @pl.loop(0, pair_count // HALF)
    def _(m):
        columns = pl.ds(pl.multiple_of(m * HALF, HALF), HALF)
        for distance in range(reach):
            table = weights[distance][0] * tab[0, :, columns]
            for slot in range(1, slots):
                table = table + weights[distance][slot] * tab[slot, :, columns]
            high = table.astype(jnp.bfloat16)
            low = (table - high.astype(jnp.float32)).astype(jnp.bfloat16)
            parts[0, distance, :, columns] = jnp.dot(place, high, preferred_element_type=jnp.float32)
            parts[1, distance, :, columns] = jnp.dot(place, low, preferred_element_type=jnp.float32)

    per_tile = EDGE // rows
    pieces = [(part, distance) for part in (0, 1, 0) for distance in range(reach)]
    lane_group = lax.broadcasted_iota(jnp.int32, (target_count, EDGE), 1) // rows

    @pl.loop(0, pair_count // EDGE)
    def _(m):
        columns = pl.ds(pl.multiple_of(m * EDGE, EDGE), EDGE)
        for r in range(per_tile):
            first = pl.multiple_of((m * per_tile + r) * target_count, target_count)
            for start in range(0, len(pieces), per_tile):
                group = pieces[start : start + per_tile]
                tile = None
                for place_at, (part, distance) in enumerate(group):
                    piece = parts[part, distance, :, columns]
                    shift = (place_at - r) * rows % EDGE
                    if shift:
                        piece = pltpu.roll(piece, shift, 1)
                    tile = piece if tile is None else jnp.where(lane_group == place_at, piece, tile)
                used = len(group) * rows
                lmat[pl.ds(first, target_count), pl.ds(start * rows, used)] = tile[:, :used].astype(
                    jnp.bfloat16
                )

    self_weight = jnp.float32(0.0)
    spill_weights = []
    for group in range(group_count):
        self_weight = self_weight + jnp.where((g == group) & (overflow[group] == g), 1.0, 0.0)
    for distance in (1, 2):
        weight = jnp.float32(0.0)
        for group in range(group_count):
            weight = weight + jnp.where((g - distance == group) & (overflow[group] == g), 1.0, 0.0)
        spill_weights.append(RATE * weight)

    block_rows = 4
    @pl.loop(0, chunks)
    def _(c):
        k = lax.rem(c + 1, chunks)
        for distance in range(1, reach):

            @pl.when(g >= distance)
            def _():
                adv_direct(distance, k).wait_recv()
                if distance + 1 < reach:

                    @pl.when(sends_sib(distance + 1))
                    def _():
                        adv_sib(distance + 1, k).start()

        for h in range(CHUNK // HALF):
            cells = pl.ds(pl.multiple_of(k * CHUNK + h * HALF, HALF), HALF)
            highs, lows = [], []
            for distance in range(reach):
                value = adv[distance, :, cells]
                high = value.astype(jnp.bfloat16)
                highs.append(high)
                lows.append((value - high.astype(jnp.float32)).astype(jnp.bfloat16))
            stack = jnp.concatenate(highs + highs + lows, axis=0)
            total = jnp.zeros((target_count, HALF), jnp.float32)
            for block in range(rows // block_rows):
                first = block * block_rows * target_count
                partial = jnp.dot(
                    lmat[pl.ds(first, block_rows * target_count), :], stack,
                    preferred_element_type=jnp.float32,
                )
                for r in range(block_rows):
                    own_row = adv[0, pl.ds(block * block_rows + r, 1), cells]
                    total = total + own_row * partial[r * target_count : (r + 1) * target_count]
            spill[0, :, cells] = total[rows:]
            out[:, cells] = adv[0, :, cells] + RATE * (total[:rows] + self_weight * total[rows:])
        for distance in (1, 2):

            @pl.when(spills_direct(distance))
            def _():
                spill_direct(distance, k).start()

        @pl.when(spills_sib(1))
        def _():
            spill_sib(1, k).start()

    @pl.loop(0, chunks)
    def _(c):
        k = lax.rem(c + 1, chunks)
        for distance in (1, 2):

            @pl.when(spill_arrives(distance))
            def _():
                spill_direct(distance, k).wait_recv()
                if distance == 1:

                    @pl.when(spills_sib(2))
                    def _():
                        spill_sib(2, k).start()

                out[:, window(k)] += spill_weights[distance - 1] * spill[distance, :, window(k)]

    @pl.when(has_right)
    def _():
        to_right.wait_send()

    @pl.when(has_left)
    def _():
        to_left.wait_send()
        speed_left.wait_send()

    @pl.loop(0, chunks)
    def _(k):
        for copy, sends, most in (
            (adv_direct, sends_direct, span),
            (adv_sib, sends_sib, span),
            (spill_direct, spills_direct, 2),
            (spill_sib, spills_sib, 2),
        ):
            for distance in range(1, most + 1):

                @pl.when(sends(distance))
                def _():
                    copy(distance, k).wait_send()


def per_device(density, courant, gain_tables, sources, counts, targets, overflow):
    rows, width = density.shape
    slots, target_count, pair_count = gain_tables.shape[1:]
    group_count = overflow.shape[0]
    span = lax.axis_size("bins") // 2
    reach = span + 1
    chunks = width // CHUNK
    anywhere = pl.BlockSpec(memory_space=pl.ANY)
    scalars = pl.BlockSpec(memory_space=pltpu.SMEM)
    vectors = pl.BlockSpec(memory_space=pltpu.VMEM)
    dma = pltpu.SemaphoreType.DMA
    return pl.pallas_call(
        functools.partial(kernel, span, group_count, lax.axis_size("blk")),
        out_shape=jax.ShapeDtypeStruct((rows, width), jnp.float32),
        in_specs=[anywhere, anywhere, anywhere, scalars, scalars, vectors, scalars],
        out_specs=vectors,
        scratch_shapes=[
            pltpu.VMEM((rows, width + 2 * EDGE), jnp.float32),
            pltpu.VMEM((rows, width + 2 * EDGE), jnp.float32),
            pltpu.VMEM((slots, target_count, pair_count), jnp.float32),
            pltpu.VMEM((reach, rows, width), jnp.float32),
            pltpu.VMEM((3, rows, width), jnp.float32),
            pltpu.VMEM((2, reach, target_count, pair_count), jnp.float32),
            pltpu.VMEM((rows * target_count, 3 * reach * rows), jnp.bfloat16),
            dma((3,)), dma((3,)), dma((3,)),
            dma((span, chunks)), dma((span, chunks)), dma((span, chunks)),
            dma((2, chunks)), dma((2, chunks)), dma((2, chunks)),
        ],
        compiler_params=pltpu.CompilerParams(
            collective_id=0, has_side_effects=True, vmem_limit_bytes=48 * 1024 * 1024
        ),
        name="drift_coagulate",
    )(density, courant, gain_tables, sources, counts, targets, overflow)


def solution(mesh):
    in_specs = (
        P("bins", "blk"),
        P("bins", "blk"),
        P("bins", None, None, None),
        P("bins", None),
        P("bins"),
        P("bins", None),
        P(),
    )
    return jax.shard_map(
        per_device, mesh=mesh, in_specs=in_specs, out_specs=P("bins", "blk"), check_vma=False
    )
```

```python
import functools

import jax
import jax.numpy as jnp
from jax import lax
from jax.experimental import pallas as pl
from jax.experimental.pallas import tpu as pltpu
from jax.sharding import PartitionSpec as P

RATE = 0.5
EDGE = 128
CHUNK = 1024
HALF = 256
MESH = pl.DeviceIdType.MESH


def minmod(first, second):
    agree = first * second > 0.0
    smaller = jnp.where(first > 0.0, jnp.minimum(first, second), jnp.maximum(first, second))
    return jnp.where(agree, smaller, jnp.zeros_like(first))


def advect_window(cells, speeds):
    width = cells.shape[1]
    diff = cells - pltpu.roll(cells, 1, 1)
    slopes = minmod(diff, pltpu.roll(diff, width - 1, 1))
    left_state = pltpu.roll(cells + 0.5 * slopes, 1, 1)
    right_state = cells - 0.5 * slopes
    flux = jnp.where(speeds > 0.0, speeds * left_state, speeds * right_state)
    moved = cells - (pltpu.roll(flux, width - 1, 1) - flux)
    return moved[:, EDGE : width - EDGE]


def kernel(
    span, group_count, blk_count,
    density, courant, tables, sources_in, counts_in, targets_in, overflow_in,
    out,
    sources, counts, targets, overflow, dpad, upad, tab, adv, spill, parts, lmat, lrest,
    load_sem, halo_send, halo_recv, direct_sem, sib_sem, adv_recv,
    sdirect_sem, ssib_sem, spill_recv,
):
    g = lax.axis_index("bins")
    b = lax.axis_index("blk")
    rows, width = density.shape
    chunks = width // CHUNK
    slots = tables.shape[1]
    target_count = tables.shape[2]
    reach = span + 1
    even = lax.rem(g, 2) == 0
    has_left, has_right = b > 0, b < blk_count - 1

    loads = [
        pltpu.make_async_copy(density, dpad.at[:, pl.ds(EDGE, width)], load_sem.at[0]),
        pltpu.make_async_copy(courant, upad.at[:, pl.ds(EDGE, width)], load_sem.at[1]),
        pltpu.make_async_copy(tables.at[0], tab, load_sem.at[2]),
        pltpu.make_async_copy(sources_in, sources, load_sem.at[3]),
        pltpu.make_async_copy(counts_in, counts, load_sem.at[4]),
        pltpu.make_async_copy(targets_in, targets, load_sem.at[5]),
        pltpu.make_async_copy(overflow_in, overflow, load_sem.at[6]),
    ]
    for load in loads:
        load.start()

    barrier = pltpu.get_barrier_semaphore()
    expected = jnp.int32(0)
    for step in [s for s in range(-span, span + 1) if s != 0]:
        there = (g + step >= 0) & (g + step < group_count)
        expected = expected + there.astype(jnp.int32)

        @pl.when(there)
        def _():
            pl.semaphore_signal(barrier, inc=1, device_id={"bins": g + step}, device_id_type=MESH)

    for step, there in ((-1, has_left), (1, has_right)):
        expected = expected + there.astype(jnp.int32)

        @pl.when(there)
        def _():
            pl.semaphore_signal(barrier, inc=1, device_id={"blk": b + step}, device_id_type=MESH)

    zero_edge = jnp.zeros((rows, EDGE), jnp.float32)
    upad[:, pl.ds(0, EDGE)] = zero_edge

    @pl.when(jnp.logical_not(has_left))
    def _():
        dpad[:, pl.ds(0, EDGE)] = zero_edge

    @pl.when(jnp.logical_not(has_right))
    def _():
        dpad[:, pl.ds(EDGE + width, EDGE)] = zero_edge
        upad[:, pl.ds(EDGE + width, EDGE)] = zero_edge

    for distance in range(1, reach):

        @pl.when(g < distance)
        def _():
            adv[distance] = jnp.zeros((rows, width), jnp.float32)

    pl.semaphore_wait(barrier, expected)

    def remote(src, dst, send, recv, where):
        return pltpu.make_async_remote_copy(
            src_ref=src, dst_ref=dst, send_sem=send, recv_sem=recv,
            device_id=where, device_id_type=MESH,
        )

    to_right = remote(
        density.at[:, pl.ds(width - EDGE, EDGE)], dpad.at[:, pl.ds(0, EDGE)],
        halo_send.at[0], halo_recv.at[0], {"blk": b + 1},
    )
    to_left = remote(
        density.at[:, pl.ds(0, EDGE)], dpad.at[:, pl.ds(EDGE + width, EDGE)],
        halo_send.at[1], halo_recv.at[1], {"blk": b - 1},
    )
    speed_left = remote(
        courant.at[:, pl.ds(0, EDGE)], upad.at[:, pl.ds(EDGE + width, EDGE)],
        halo_send.at[2], halo_recv.at[2], {"blk": b - 1},
    )

    @pl.when(has_right)
    def _():
        to_right.start()

    @pl.when(has_left)
    def _():
        to_left.start()
        speed_left.start()

    def window(k):
        return pl.ds(pl.multiple_of(k * CHUNK, CHUNK), CHUNK)

    def adv_direct(distance, k):
        return remote(
            adv.at[0, :, window(k)], adv.at[distance, :, window(k)],
            direct_sem.at[distance - 1, k], adv_recv.at[distance - 1, k], {"bins": g + distance},
        )

    def adv_sib(distance, k):
        return remote(
            adv.at[distance - 1, :, window(k)], adv.at[distance, :, window(k)],
            sib_sem.at[distance - 1, k], adv_recv.at[distance - 1, k], {"bins": g + 1},
        )

    def spill_direct(distance, k):
        return remote(
            spill.at[0, :, window(k)], spill.at[distance, :, window(k)],
            sdirect_sem.at[distance - 1, k], spill_recv.at[distance - 1, k], {"bins": g + distance},
        )

    def spill_sib(distance, k):
        return remote(
            spill.at[distance - 1, :, window(k)], spill.at[distance, :, window(k)],
            ssib_sem.at[distance - 1, k], spill_recv.at[distance - 1, k], {"bins": g + 1},
        )

    def sends_direct(distance):
        target = g + distance
        return (target < group_count) & (lax.rem(target, 2) == 0)

    def sends_sib(distance):
        return even & (g + 1 < group_count) & (g >= distance - 1)

    def spills_direct(distance):
        target = g + distance
        fits = (target < group_count) & (lax.rem(target, 2) == 0)
        return fits & (g > 0) if distance > 1 else fits

    def spills_sib(distance):
        fits = even & (g + 1 < group_count)
        return fits & (g > 1) if distance > 1 else fits

    def spill_arrives(distance):
        return g >= (1 if distance == 1 else 3)

    loads[0].wait()
    loads[1].wait()

    @pl.loop(0, chunks)
    def _(c):
        k = lax.rem(c + 1, chunks)

        @pl.when(c == chunks - 2)
        def _():
            @pl.when(has_left)
            def _():
                to_right.wait_recv()

            @pl.when(has_right)
            def _():
                to_left.wait_recv()
                speed_left.wait_recv()

        padded = pl.ds(pl.multiple_of(k * CHUNK, CHUNK), CHUNK + 2 * EDGE)
        adv[0, :, window(k)] = advect_window(dpad[:, padded], upad[:, padded])
        for distance in range(1, reach):

            @pl.when(sends_direct(distance))
            def _():
                adv_direct(distance, k).start()

        @pl.when(sends_sib(1))
        def _():
            adv_sib(1, k).start()

    for load in loads[2:]:
        load.wait()
    place = (
        lax.broadcasted_iota(jnp.int32, (target_count, target_count), 0) == targets[...]
    ).astype(jnp.float32).astype(jnp.bfloat16)
    weights = [
        [
            jnp.where((sources[0, slot] == g - distance) & (slot < counts[0]), 1.0, 0.0)
            for slot in range(slots)
        ]
        for distance in range(reach)
    ]
    pair_count = tab.shape[2]

    @pl.loop(0, pair_count // HALF)
    def _(m):
        columns = pl.ds(pl.multiple_of(m * HALF, HALF), HALF)
        for distance in range(reach):
            table = weights[distance][0] * tab[0, :, columns]
            for slot in range(1, slots):
                table = table + weights[distance][slot] * tab[slot, :, columns]
            high = table.astype(jnp.bfloat16)
            low = (table - high.astype(jnp.float32)).astype(jnp.bfloat16)
            parts[0, distance, :, columns] = jnp.dot(place, high, preferred_element_type=jnp.float32)
            parts[1, distance, :, columns] = jnp.dot(place, low, preferred_element_type=jnp.float32)

            if distance == span:
                lrest[:, columns] = parts[0, distance, :, columns].astype(jnp.bfloat16)

    per_tile = EDGE // rows
    pieces = [(part, distance) for part in (0, 1, 0) for distance in range(reach)][:-1]
    lane_group = lax.broadcasted_iota(jnp.int32, (target_count, EDGE), 1) // rows

    @pl.loop(0, pair_count // EDGE)
    def _(m):
        columns = pl.ds(pl.multiple_of(m * EDGE, EDGE), EDGE)
        for r in range(per_tile):
            first = pl.multiple_of((m * per_tile + r) * target_count, target_count)
            for start in range(0, len(pieces), per_tile):
                group = pieces[start : start + per_tile]
                tile = None
                for place_at, (part, distance) in enumerate(group):
                    piece = parts[part, distance, :, columns]
                    shift = (place_at - r) * rows % EDGE
                    if shift:
                        piece = pltpu.roll(piece, shift, 1)
                    tile = piece if tile is None else jnp.where(lane_group == place_at, piece, tile)
                used = len(group) * rows
                lmat[pl.ds(first, target_count), pl.ds(start * rows, used)] = tile[:, :used].astype(
                    jnp.bfloat16
                )

    self_weight = jnp.float32(0.0)
    spill_weights = []
    for group in range(group_count):
        self_weight = self_weight + jnp.where((g == group) & (overflow[group] == g), 1.0, 0.0)
    for distance in (1, 2):
        weight = jnp.float32(0.0)
        for group in range(group_count):
            weight = weight + jnp.where((g - distance == group) & (overflow[group] == g), 1.0, 0.0)
        spill_weights.append(RATE * weight)

    block_rows = 8
    @pl.loop(0, chunks)
    def _(c):
        k = lax.rem(c + 1, chunks)
        for distance in range(1, reach):

            @pl.when(g >= distance)
            def _():
                adv_direct(distance, k).wait_recv()
                if distance + 1 < reach:

                    @pl.when(sends_sib(distance + 1))
                    def _():
                        adv_sib(distance + 1, k).start()

        for h in range(CHUNK // HALF):
            cells = pl.ds(pl.multiple_of(k * CHUNK + h * HALF, HALF), HALF)
            highs, lows = [], []
            for distance in range(reach):
                value = adv[distance, :, cells]
                high = value.astype(jnp.bfloat16)
                highs.append(high)
                lows.append((value - high.astype(jnp.float32)).astype(jnp.bfloat16))
            stack = jnp.concatenate(highs + highs + lows[:-1], axis=0)
            last_low = lows[-1].astype(jnp.float32)
            total = jnp.zeros((target_count, HALF), jnp.float32)
            for block in range(rows // block_rows):
                first = block * block_rows * target_count
                partial = jnp.dot(
                    lmat[pl.ds(first, block_rows * target_count), :], stack,
                    preferred_element_type=jnp.float32,
                )
                outer = []
                for r in range(block_rows):
                    own_row = adv[0, pl.ds(block * block_rows + r, 1), cells]
                    total = total + own_row * partial[r * target_count : (r + 1) * target_count]
                    outer.append((own_row * last_low).astype(jnp.bfloat16))
                pairs = pl.ds(block * block_rows * rows, block_rows * rows)
                total = total + jnp.dot(
                    lrest[:, pairs], jnp.concatenate(outer, axis=0),
                    preferred_element_type=jnp.float32,
                )
            spill[0, :, cells] = total[rows:]
            out[:, cells] = adv[0, :, cells] + RATE * (total[:rows] + self_weight * total[rows:])
        for distance in (1, 2):

            @pl.when(spills_direct(distance))
            def _():
                spill_direct(distance, k).start()

        @pl.when(spills_sib(1))
        def _():
            spill_sib(1, k).start()

    @pl.loop(0, chunks)
    def _(c):
        k = lax.rem(c + 1, chunks)
        for distance in (1, 2):

            @pl.when(spill_arrives(distance))
            def _():
                spill_direct(distance, k).wait_recv()
                if distance == 1:

                    @pl.when(spills_sib(2))
                    def _():
                        spill_sib(2, k).start()

                out[:, window(k)] += spill_weights[distance - 1] * spill[distance, :, window(k)]

    @pl.when(has_right)
    def _():
        to_right.wait_send()

    @pl.when(has_left)
    def _():
        to_left.wait_send()
        speed_left.wait_send()

    @pl.loop(0, chunks)
    def _(k):
        for copy, sends, most in (
            (adv_direct, sends_direct, span),
            (adv_sib, sends_sib, span),
            (spill_direct, spills_direct, 2),
            (spill_sib, spills_sib, 2),
        ):
            for distance in range(1, most + 1):

                @pl.when(sends(distance))
                def _():
                    copy(distance, k).wait_send()


def per_device(density, courant, gain_tables, sources, counts, targets, overflow):
    rows, width = density.shape
    slots, target_count, pair_count = gain_tables.shape[1:]
    group_count = overflow.shape[0]
    span = lax.axis_size("bins") // 2
    reach = span + 1
    chunks = width // CHUNK
    main = pl.BlockSpec(memory_space=pltpu.HBM)
    vectors = pl.BlockSpec(memory_space=pltpu.VMEM)
    dma = pltpu.SemaphoreType.DMA
    return pl.pallas_call(
        functools.partial(kernel, span, group_count, lax.axis_size("blk")),
        out_shape=jax.ShapeDtypeStruct((rows, width), jnp.float32),
        in_specs=[main] * 7,
        out_specs=vectors,
        scratch_shapes=[
            pltpu.SMEM(sources.shape, jnp.int32),
            pltpu.SMEM(counts.shape, jnp.int32),
            pltpu.VMEM(targets.shape, jnp.int32),
            pltpu.SMEM(overflow.shape, jnp.int32),
            pltpu.VMEM((rows, width + 2 * EDGE), jnp.float32),
            pltpu.VMEM((rows, width + 2 * EDGE), jnp.float32),
            pltpu.VMEM((slots, target_count, pair_count), jnp.float32),
            pltpu.VMEM((reach, rows, width), jnp.float32),
            pltpu.VMEM((3, rows, width), jnp.float32),
            pltpu.VMEM((2, reach, target_count, pair_count), jnp.float32),
            pltpu.VMEM((rows * target_count, (3 * reach - 1) * rows), jnp.bfloat16),
            pltpu.VMEM((target_count, pair_count), jnp.bfloat16),
            dma((7,)), dma((3,)), dma((3,)),
            dma((span, chunks)), dma((span, chunks)), dma((span, chunks)),
            dma((2, chunks)), dma((2, chunks)), dma((2, chunks)),
        ],
        compiler_params=pltpu.CompilerParams(
            collective_id=0, has_side_effects=True, vmem_limit_bytes=67043328
        ),
        name="drift_coagulate",
    )(density, courant, gain_tables, sources, counts, targets, overflow)


def solution(mesh):
    in_specs = (
        P("bins", "blk"),
        P("bins", "blk"),
        P("bins", None, None, None),
        P("bins", None),
        P("bins"),
        P("bins", None),
        P(),
    )
    return jax.shard_map(
        per_device, mesh=mesh, in_specs=in_specs, out_specs=P("bins", "blk"), check_vma=False
    )
```
